512 devices in a mesh: rep: 4 (over x), rows: 128 (over y, z, core).
Axes of the slice: x: 4, y: 4, z: 16, core: 2. Of those that a mesh axis runs over, the one named last changes fastest.
Arguments:
- features: bfloat16 [65536, 256], P('rows'), may hold values from -6 to 6
- tiles: bfloat16 [128, 4, 2, 256, 256], P('rows', 'rep'), may hold values from -0.1875 to 0.1875
- tile_row: int32 [128, 4, 2], P('rows', 'rep'), may hold values from 0 to 1, as said below
- tile_col: int32 [128, 4, 2], P('rows', 'rep'), may hold values from 0 to 3, as said below
- tile_live: int32 [128, 4], P('rows', 'rep'), may hold values from 1 to 2, as said below
- send_index: int32 [128, 128, 4], P('rows'), may hold values from 0 to 511
- gain: float32 [3, 256], replicated, may hold values from 0.1 to 1.9
- w_in: bfloat16 [3, 256, 512], replicated, may hold values from -0.375 to 0.375
- w_out: bfloat16 [3, 512, 256], replicated, may hold values from -0.25 to 0.25
Outputs:
- result: bfloat16 [65536, 256], P('rows')
The draws below stay inside these ranges and needn't reach their ends.
Inputs may be any that keep to these rules, and one draw needn't show every extreme that they name: `tile_live`: every owner and section has at least one slot in use, and some owner and section has all 2. For each owner, the pairs (tile_row, tile_col) over all sections and slots are all different. For each owner, the pairs (tile_row, tile_col) over all sections and slots are all different.
All inputs are finite; a program needn't handle non-finite values.
Results may differ from the reference program's by a relative error of at most 0.012.
Values may be sent and summed in bfloat16 or wider, within the bound.
A program may use at most 64 MiB of HBM per device.

```python
import jax
import jax.numpy as jnp
from jax import lax

F = 256
HID = 512
TILE = 256
HOPS = 3
NODES_DEV = 512
HALO = 4
TILES_DEV = 2
OWNERS = 128
SECTIONS = 4
NODES = 65536
HALO_PAD = 512
ROW_TILES = 2
COL_TILES = 4
N_REP = 4


def draw_tile_live(key, part):
    counts = jax.random.randint(key, (OWNERS, SECTIONS), 1, TILES_DEV + 1)
    return counts.at[0, 0].set(TILES_DEV).astype(jnp.int32)


def tile_positions(key):
    base = jax.random.fold_in(key, 7)
    total = ROW_TILES * COL_TILES
    owner_keys = jax.random.split(base, OWNERS)
    orders = jax.vmap(lambda k: jax.random.permutation(k, total))(owner_keys).astype(jnp.int32)
    first = orders[0]
    where_last = jnp.argmax(first == total - 1)
    first = first.at[where_last].set(first[0]).at[0].set(total - 1)
    orders = orders.at[0].set(first)
    chosen = orders[:, :SECTIONS * TILES_DEV].reshape(OWNERS, SECTIONS, TILES_DEV)
    return chosen.astype(jnp.int32)


def draw_tile_row(key, part):
    return (tile_positions(key) // COL_TILES).astype(jnp.int32)


def draw_tile_col(key, part):
    return (tile_positions(key) % COL_TILES).astype(jnp.int32)


def place_ends(entries, rng, least, largest):
    longest = entries.shape.index(max(entries.shape))
    spots = []
    for shift in (0, 1):
        where = [jax.random.randint(jax.random.fold_in(rng, axis), (), 0, length) for axis, length in enumerate(entries.shape)]
        where[longest] = (where[longest] + shift) % entries.shape[longest]
        spots.append(tuple(where))
    return entries.at[spots[0]].set(least).at[spots[1]].set(largest)


def level_of(rng, extent, shards, low, largest):
    level = 1.0
    for position, blocks in shards:
        steps = jax.random.uniform(jax.random.fold_in(jax.random.fold_in(rng, 6), position), (blocks,), jnp.float32, low / len(shards), largest / len(shards))
        level = level * jnp.repeat(jnp.exp(steps), extent[position] // blocks).reshape((-1,) + (1,) * (len(extent) - 1 - position))
    return level


def noise(key, shape, deviation, reach, cuts=(), held_as=jnp.bfloat16):
    drawn = deviation * jax.random.normal(key, shape, jnp.float32)
    if cuts:
        drawn = drawn * level_of(key, shape, cuts, -0.22, 0.18)
    return jnp.clip(drawn, -reach, reach).astype(held_as)


def setup_inputs(seed: int = 0) -> dict:
    keys = jax.random.split(jax.random.key(seed), 10)
    return {
        "features": noise(keys[0], (NODES, F), 1.0, 6.0, ((0, 128),)),
        "tiles": noise(keys[1], (OWNERS, SECTIONS, TILES_DEV, TILE, TILE), (TILE * TILES_DEV * N_REP // ROW_TILES) ** -0.5, 0.1875, ((0, 128), (1, 4))),
        "tile_row": draw_tile_row(jax.random.fold_in(keys[9], 71), 0),
        "tile_col": draw_tile_col(jax.random.fold_in(keys[9], 71), 0),
        "tile_live": draw_tile_live(jax.random.fold_in(keys[9], 71), 0),
        "send_index": place_ends(jax.random.randint(keys[5], (OWNERS, OWNERS, HALO), 0, NODES_DEV), jax.random.fold_in(keys[5], 1), 0, NODES_DEV - 1).astype(jnp.int32),
        "gain": jnp.clip(1.0 + 0.18 * jax.random.normal(keys[6], (HOPS, F), jnp.float32), 0.1, 1.9),
        "w_in": noise(keys[7], (HOPS, F, HID), F ** -0.5, 0.375),
        "w_out": noise(keys[8], (HOPS, HID, F), HID ** -0.5, 0.25),
    }


def one_owner(owned, tiles_o, row_o, col_o, live_o, halo_o):
    pad_rows = jnp.zeros((HALO_PAD - OWNERS * HALO, F), jnp.float32)
    extended = jnp.concatenate([owned, halo_o.reshape(OWNERS * HALO, F), pad_rows], axis=0)
    column_tiles = extended.reshape(COL_TILES, TILE, F)
    picked = column_tiles[col_o]
    products = jnp.einsum('stij,stjf->stif', tiles_o.astype(jnp.float32), picked)
    slot_live = (jnp.arange(TILES_DEV, dtype=jnp.int32)[None, :] < live_o[:, None]).astype(jnp.float32)
    products = products * slot_live[:, :, None, None]
    onehot = (row_o[:, :, None] == jnp.arange(ROW_TILES, dtype=jnp.int32)[None, None, :]).astype(jnp.float32)
    summed = jnp.einsum('str,stif->rif', onehot, products)
    return summed.reshape(NODES_DEV, F)

def reference(features, tiles, tile_row, tile_col, tile_live, send_index, gain, w_in, w_out):
    current = features
    owner_ids = jnp.arange(OWNERS, dtype=jnp.int32)
    for step in range(HOPS):
        blocks = current.reshape(OWNERS, NODES_DEV, F).astype(jnp.float32)

        def per_owner(owner):
            rows_from = send_index[:, owner, :]
            halo_o = blocks[owner_ids[:, None], rows_from]
            return one_owner(blocks[owner], tiles[owner], tile_row[owner], tile_col[owner], tile_live[owner], halo_o)
        gathered = lax.map(per_owner, owner_ids).reshape(NODES, F)
        mixed = current.astype(jnp.float32) + gathered
        scale = lax.rsqrt(lax.optimization_barrier(jnp.mean(mixed * mixed, axis=-1, keepdims=True)) + 1e-06)
        normed = (mixed * scale * gain[step][None, :]).astype(jnp.bfloat16)
        inner = jax.nn.gelu(jnp.dot(normed, w_in[step], preferred_element_type=jnp.float32)).astype(jnp.bfloat16)
        current = (mixed + jnp.dot(inner, w_out[step], preferred_element_type=jnp.float32)).astype(jnp.bfloat16)
    return current
```

```python
import functools

import jax
import jax.numpy as jnp
from jax import lax
from jax.experimental import pallas as pl
from jax.experimental.pallas import tpu as pltpu
from jax.sharding import PartitionSpec as P

HOPS = 3
MESH = pl.DeviceIdType.MESH
BF = jnp.bfloat16
F32 = jnp.float32


def plane_of(owners):
    return {128: (4, 16, 2), 8: (2, 2, 2)}[owners]


def kernel(
    reps, owners, feat_hbm, tiles_hbm, row_ref, col_ref, live_ref, index_ref, gain_ref, win_hbm, wout_hbm,
    out_ref,
    index_t, cur, pick, sent, recv, half_mask, spread, tiles_all, marks, block, wide, total, win, wout,
    load_sem, tile_send, tile_recv, mark_send, mark_recv, halo_send, halo_recv, own_sem,
):
    ys, zs, cs = plane_of(owners)
    rep = lax.axis_index("rep")
    me = lax.axis_index("rows")
    my_y, my_z, my_c = me // (zs * cs), (me // cs) % zs, me % cs
    nodes, width = feat_hbm.shape
    side = tiles_hbm.shape[-1]
    slots = tiles_hbm.shape[0]
    halo = index_ref.shape[0]
    half = width // 2
    group = 2 * halo
    row_tiles = nodes // side
    col_tiles = block.shape[1] // side
    own_tiles = nodes // side

    barrier = pltpu.get_barrier_semaphore()

    def target(dz, dy, dc):
        y = lax.rem(my_y + dy, ys)
        z = lax.rem(my_z + dz, zs)
        c = lax.rem(my_c + dc, cs)
        return (y * zs + z) * cs + c

    def far_first(visit):
        def some(dz, skip_self):
            for dy in sorted(range(ys), key=lambda d: -min(d, ys - d)):
                for dc in reversed(range(cs)):
                    if skip_self and dy == 0 and dc == 0:
                        continue
                    visit(target(dz, dy, dc))

        @pl.loop(0, zs - 1)
        def _(j):
            some(zs // 2 + (1 - 2 * lax.rem(j, 2)) * ((j + 1) // 2), False)

        some(0, True)

    def greet(owner):
        pl.semaphore_signal(barrier, inc=1, device_id=(rep, owner), device_id_type=MESH)

    far_first(greet)
    for d in range(1, reps):
        pl.semaphore_signal(
            barrier, inc=1, device_id=(lax.rem(rep + d, reps), me), device_id_type=MESH
        )

    loads = [
        pltpu.make_async_copy(feat_hbm, cur, load_sem.at[0]),
        pltpu.make_async_copy(tiles_hbm, tiles_all.at[rep], load_sem.at[1]),
        pltpu.make_async_copy(win_hbm, win, load_sem.at[2]),
        pltpu.make_async_copy(wout_hbm, wout, load_sem.at[3]),
    ]
    for load in loads:
        load.start()

    positions = row_tiles * col_tiles
    line = lax.broadcasted_iota(jnp.int32, marks.shape[1:], 0)
    mark = jnp.zeros(marks.shape[1:], F32)
    for slot in range(slots):
        where = row_ref[slot] * col_tiles + col_ref[slot]
        where = jnp.where(slot < live_ref[0], where + slot * positions, -1)
        mark = jnp.where(line == where, 1.0, mark)
    marks[rep] = mark

    per = 16 // group
    wide_index = jnp.concatenate([index_ref[...]] * 2, axis=0)
    index_t[...] = jnp.transpose(wide_index)
    lane = lax.broadcasted_iota(jnp.int32, (group, group), 1)
    sub = lax.broadcasted_iota(jnp.int32, (group, group), 0)
    node = lax.broadcasted_iota(jnp.int32, (group, nodes), 1)
    for o in range(0, owners, per):
        rows = []
        for q in range(per):
            wanted = jnp.broadcast_to(index_t[o + q : o + q + 1, :], (group, group))
            wanted = jnp.sum(jnp.where(lane == sub, wanted, 0), axis=1, keepdims=True)
            rows.append(jnp.where(node == wanted, 1.0, 0.0).astype(F32))
        pick[o * group : (o + per) * group, :] = jnp.concatenate(rows, axis=0).astype(BF)
    total_lines = owners * group
    lines = lax.broadcasted_iota(jnp.int32, (total_lines, half), 0)
    half_mask[...] = jnp.where(lax.rem(lines, group) < halo, 1.0, 0.0).astype(BF)
    at = lax.broadcasted_iota(jnp.int32, spread.shape, 0)
    to = lax.broadcasted_iota(jnp.int32, spread.shape, 1)
    same = (at // halo == to // group) & (lax.rem(at, halo) == lax.rem(to, halo))
    spread[...] = jnp.where(same, 1.0, 0.0).astype(BF)

    loads[0].wait()

    def gather(hop):
        step = min(256, total_lines)
        for first in range(0, total_lines, step):
            got = jnp.dot(pick[first : first + step, :], cur[...], preferred_element_type=F32)
            line = lax.rem(lax.broadcasted_iota(jnp.int32, (step, half), 0), group)
            message = jnp.where(line < halo, got[:, :half], got[:, half:])
            sent[hop, first // group : (first + step) // group] = message.astype(BF).reshape(
                step // group, group, half
            )

    def exchange(hop):
        def send(owner):
            pltpu.make_async_remote_copy(
                src_ref=sent.at[hop, owner],
                dst_ref=recv.at[hop, me],
                send_sem=halo_send.at[hop],
                recv_sem=halo_recv.at[hop],
                device_id=(rep, owner),
                device_id_type=MESH,
            ).start()

        far_first(send)
        pltpu.make_async_copy(sent.at[hop, me], recv.at[hop, me], own_sem.at[hop]).start()

    gather(0)
    pl.semaphore_wait(barrier, owners - 1 + reps - 1)
    exchange(0)
    for d in range(1, reps):
        peer = (lax.rem(rep + d, reps), me)
        pltpu.make_async_remote_copy(
            src_ref=marks.at[rep], dst_ref=marks.at[rep], send_sem=mark_send, recv_sem=mark_recv,
            device_id=peer, device_id_type=MESH,
        ).start()
        pltpu.make_async_remote_copy(
            src_ref=tiles_hbm, dst_ref=tiles_all.at[rep], send_sem=tile_send, recv_sem=tile_recv,
            device_id=peer, device_id_type=MESH,
        ).start()

    for load in loads[1:]:
        load.wait()
    others = pl.ds(0, reps - 1)
    pltpu.make_async_copy(marks.at[others], marks.at[others], mark_recv).wait()
    pltpu.make_async_copy(tiles_all.at[others], tiles_all.at[others], tile_recv).wait()

    chunk = 64
    for r in range(row_tiles):
        for c in range(col_tiles):

            @pl.loop(0, side // chunk)
            def _(i):
                at = pl.ds(pl.multiple_of(i * chunk, chunk), chunk)
                to = pl.ds(pl.multiple_of(r * side + i * chunk, chunk), chunk)
                value = jnp.zeros((chunk, side), F32)
                for s in range(reps):
                    for slot in range(slots):
                        which = slot * positions + r * col_tiles + c
                        here = marks[s, which : which + 1, :]
                        here = jnp.concatenate([here] * (side // here.shape[1]), axis=1)
                        value += tiles_all[s, slot, at, :].astype(F32) * here
                block[to, c * side : (c + 1) * side] = value.astype(BF)

    for c in range(own_tiles, col_tiles):
        q = c - own_tiles
        columns = min(2 * side, wide.shape[1])
        wide[:, q * 2 * side : q * 2 * side + columns] = jnp.dot(
            block[:, c * side : (c + 1) * side], spread[:, :columns], preferred_element_type=F32
        ).astype(BF)

    rows = 256
    for hop in range(HOPS):
        if hop:
            gather(hop)
            exchange(hop)
        for first in range(0, nodes, rows):
            total[first : first + rows, :] = jnp.dot(
                block[first : first + rows, :nodes], cur[...], preferred_element_type=F32
            ) + cur[first : first + rows, :].astype(F32)
        pltpu.make_async_copy(sent.at[hop, me], recv.at[hop, me], own_sem.at[hop]).wait()
        arrived = recv.at[hop, pl.ds(0, owners - 1)]
        pltpu.make_async_copy(arrived, arrived, halo_recv.at[hop]).wait()
        came = recv[hop].reshape(total_lines, half)
        low = came * half_mask[...]
        both = jnp.concatenate([low, came - low], axis=1)
        for first in range(0, nodes, rows):
            here = slice(first, first + rows)
            mixed = total[here, :] + jnp.dot(wide[here, :], both, preferred_element_type=F32)
            scale = lax.rsqrt(jnp.mean(mixed * mixed, axis=-1, keepdims=True) + 1e-06)
            normed = (mixed * scale * gain_ref[hop : hop + 1, :]).astype(BF)
            inner = jax.nn.gelu(jnp.dot(normed, win[hop], preferred_element_type=F32)).astype(BF)
            result = (mixed + jnp.dot(inner, wout[hop], preferred_element_type=F32)).astype(BF)
            if hop == HOPS - 1:
                out_ref[here, :] = result
            else:
                cur[here, :] = result

    for hop in range(HOPS):
        left = sent.at[hop, pl.ds(0, owners - 1)]
        pltpu.make_async_copy(left, left, halo_send.at[hop]).wait()
    pltpu.make_async_copy(marks.at[others], marks.at[others], mark_send).wait()
    pltpu.make_async_copy(tiles_all.at[others], tiles_all.at[others], tile_send).wait()


def per_device(reps, owners, features, tiles, tile_row, tile_col, tile_live, send_index, gain, w_in, w_out):
    nodes, width = features.shape
    slots, side = tiles.shape[2], tiles.shape[-1]
    halo = send_index.shape[2]
    halo_pad = (owners * halo + side - 1) // side * side
    columns = nodes + halo_pad
    lines = owners * 2 * halo
    positions = (nodes // side) * (columns // side)
    mark_lines = (slots * positions + 7) // 8 * 8
    smem = pl.BlockSpec(memory_space=pltpu.SMEM)
    vmem = pl.BlockSpec(memory_space=pltpu.VMEM)
    hbm = pl.BlockSpec(memory_space=pl.ANY)
    dma = pltpu.SemaphoreType.DMA
    return pl.pallas_call(
        functools.partial(kernel, reps, owners),
        out_shape=jax.ShapeDtypeStruct((nodes, width), BF),
        in_specs=[hbm, hbm, smem, smem, smem, vmem, vmem, hbm, hbm],
        out_specs=vmem,
        scratch_shapes=[
            pltpu.VMEM((owners, 2 * halo), jnp.int32),
            pltpu.VMEM((nodes, width), BF),
            pltpu.VMEM((lines, nodes), BF),
            pltpu.VMEM((HOPS, owners, 2 * halo, width // 2), BF),
            pltpu.VMEM((HOPS, owners, 2 * halo, width // 2), BF),
            pltpu.VMEM((lines, width // 2), BF),
            pltpu.VMEM((side, 2 * side), BF),
            pltpu.VMEM((reps, slots, side, side), BF),
            pltpu.VMEM((reps, mark_lines, 128), F32),
            pltpu.VMEM((nodes, columns), BF),
            pltpu.VMEM((nodes, lines), BF),
            pltpu.VMEM((nodes, width), F32),
            pltpu.VMEM(w_in.shape, BF),
            pltpu.VMEM(w_out.shape, BF),
            dma((4,)),
            dma, dma, dma, dma,
            dma((HOPS,)),
            dma((HOPS,)),
            dma((HOPS,)),
        ],
        compiler_params=pltpu.CompilerParams(
            collective_id=0, has_side_effects=True, vmem_limit_bytes=60 * 1024 * 1024
        ),
    )(
        features, tiles[0, 0], tile_row[0, 0], tile_col[0, 0], tile_live[0], jnp.transpose(send_index[0]), gain, w_in, w_out
    )


def solution(mesh):
    placed = (
        P("rows", None),
        P("rows", "rep", None, None, None),
        P("rows", "rep", None),
        P("rows", "rep", None),
        P("rows", "rep"),
        P("rows", None, None),
        P(),
        P(),
        P(),
    )
    body = functools.partial(per_device, mesh.shape["rep"], mesh.shape["rows"])
    return jax.shard_map(body, mesh=mesh, in_specs=placed, out_specs=P("rows", None), check_vma=False)
```

```python
import functools

import jax
import jax.numpy as jnp
from jax import lax
from jax.experimental import pallas as pl
from jax.experimental.pallas import tpu as pltpu
from jax.sharding import PartitionSpec as P

HOPS = 3
DIRECT = 0
BATCHES = ((0, 3), (3, 7), (7, 11), (11, 16))
FOLDED_FIRST = True
MESH = pl.DeviceIdType.MESH
BF = jnp.bfloat16
F32 = jnp.float32


def plane_of(owners):
    return {128: (4, 16, 2), 8: (2, 2, 2), 4: (4, 1, 1)}[owners]


def batches_of(zs):
    if zs == 16:
        return DIRECT, BATCHES
    return min(1, zs - 1), ((min(1, zs - 1), zs),)


def kernel(
    reps, owners, feat_hbm, tiles_hbm, row_hbm, col_hbm, live_hbm, index_hbm, gain_hbm, win_hbm, wout_hbm,
    out_ref,
    row_ref, col_ref, live_ref, index_ref, gain_ref,
    index_t, cur, pick, sent, recv, half_mask, spread, tiles_all, marks, block, wide, total, win, wout,
    load_sem, tile_send, tile_recv, mark_send, mark_recv, halo_send, halo_recv, fold_send, fold_recv,
):
    ys, zs, cs = plane_of(owners)
    direct, batches = batches_of(zs)
    rep = lax.axis_index("rep")
    me = lax.axis_index("rows")
    my_y, my_z, my_c = me // (zs * cs), (me // cs) % zs, me % cs
    nodes, width = feat_hbm.shape
    side = tiles_hbm.shape[-1]
    slots = tiles_hbm.shape[0]
    halo = index_hbm.shape[0]
    half = width // 2
    group = 2 * halo
    row_tiles = nodes // side
    col_tiles = block.shape[1] // side
    own_tiles = nodes // side
    far_y = sorted(range(ys), key=lambda d: -min(d, ys - d))
    far_x = sorted(range(1, reps), key=lambda d: -min(d, reps - d))

    barrier = pltpu.get_barrier_semaphore()

    def at(sign, dz, dy, dc):
        y = lax.rem(my_y + sign * dy + ys, ys)
        z = lax.rem(my_z + sign * dz + zs, zs)
        c = lax.rem(my_c + sign * dc + cs, cs)
        return (y * zs + z) * cs + c

    def step_of(j):
        return zs // 2 + (1 - 2 * lax.rem(j, 2)) * ((j + 1) // 2)

    def my_dy(dz):
        return lax.rem(rep + ys * zs - dz, ys)

    def partners(sign, visit):
        def whole():
            @pl.loop(0, direct)
            def _(j):
                dz = step_of(j)
                for dy in far_y:
                    for dc in reversed(range(cs)):
                        visit(at(sign, dz, dy, dc), 0)

        if direct and not FOLDED_FIRST:
            whole()
        for b, (low, high) in enumerate(batches):
            if min(high, zs - 1) > low:

                @pl.loop(low, min(high, zs - 1))
                def _(j, b=b):
                    dz = step_of(j)
                    for dc in reversed(range(cs)):
                        visit(at(sign, dz, my_dy(dz), dc), b + 1)

        for dc in reversed(range(1, cs)):
            visit(at(sign, 0, my_dy(0), dc), len(batches))

        @pl.when(rep != 0)
        def _():
            visit(at(sign, 0, my_dy(0), 0), len(batches))

        if direct and FOLDED_FIRST:
            whole()

    def greet(owner, _):
        pl.semaphore_signal(barrier, inc=1, device_id=(rep, owner), device_id_type=MESH)

    partners(-1, greet)
    for d in far_x:
        pl.semaphore_signal(
            barrier, inc=1, device_id=(lax.rem(rep + d, reps), me), device_id_type=MESH
        )
    messages = direct * ys * cs + (zs - direct) * cs

    loads = [
        pltpu.make_async_copy(source, to, load_sem.at[n])
        for n, (source, to) in enumerate(
            (
                (index_hbm, index_ref), (feat_hbm, cur), (row_hbm, row_ref), (col_hbm, col_ref), (live_hbm, live_ref),
                (tiles_hbm, tiles_all.at[rep]), (gain_hbm, gain_ref), (win_hbm, win), (wout_hbm, wout),
            )
        )
    ]
    for load in loads:
        load.start()

    total_lines = owners * group
    lines = lax.broadcasted_iota(jnp.int32, (total_lines, half), 0)
    half_mask[...] = jnp.where(lax.rem(lines, group) < halo, 1.0, 0.0).astype(BF)
    x = lax.broadcasted_iota(jnp.int32, spread.shape, 0)
    y = lax.broadcasted_iota(jnp.int32, spread.shape, 1)
    same = (x // halo == y // group) & (lax.rem(x, halo) == lax.rem(y, halo))
    spread[...] = jnp.where(same, 1.0, 0.0).astype(BF)

    loads[0].wait()
    per = 16 // group
    index_t[...] = jnp.transpose(jnp.concatenate([index_ref[...]] * 2, axis=0))
    lane = lax.broadcasted_iota(jnp.int32, (group, group), 1)
    sub = lax.broadcasted_iota(jnp.int32, (group, group), 0)
    node = lax.broadcasted_iota(jnp.int32, (group, nodes), 1)
    for o in range(0, owners, per):
        rows = []
        for q in range(per):
            wanted = jnp.broadcast_to(index_t[o + q : o + q + 1, :], (group, group))
            wanted = jnp.sum(jnp.where(lane == sub, wanted, 0), axis=1, keepdims=True)
            rows.append(jnp.where(node == wanted, 1.0, 0.0).astype(F32))
        pick[o * group : (o + per) * group, :] = jnp.concatenate(rows, axis=0).astype(BF)

    loads[1].wait()

    def gather(hop):
        step = min(256, total_lines)
        for first in range(0, total_lines, step):
            got = jnp.dot(pick[first : first + step, :], cur[...], preferred_element_type=F32)
            line = lax.rem(lax.broadcasted_iota(jnp.int32, (step, half), 0), group)
            message = jnp.where(line < halo, got[:, :half], got[:, half:])
            sent[hop, first // group : (first + step) // group] = message.astype(BF).reshape(
                step // group, group, half
            )

    def exchange(hop):
        def send(owner, b):
            pltpu.make_async_remote_copy(
                src_ref=sent.at[hop, owner],
                dst_ref=recv.at[hop, me],
                send_sem=halo_send.at[hop],
                recv_sem=halo_recv.at[hop, b],
                device_id=(rep, owner),
                device_id_type=MESH,
            ).start()

        partners(1, send)

        @pl.when(rep == 0)
        def _():
            pltpu.make_async_copy(
                sent.at[hop, me], recv.at[hop, me], halo_recv.at[hop, len(batches)]
            ).start()

    def settle(ref, sem):
        pltpu.make_async_copy(ref, ref, sem).wait()

    def fold(hop, b):
        low, high = batches[b]
        settle(recv.at[hop, pl.ds(0, (high - low) * cs)], halo_recv.at[hop, b + 1])

        @pl.loop(low, high)
        def _(j):
            dz = step_of(j)
            y = lax.rem(my_y - my_dy(dz) + ys, ys)
            z = lax.rem(my_z - dz + zs, zs)
            pair = recv.at[hop, pl.ds((y * zs + z) * cs, cs)]
            for d in far_x:
                pltpu.make_async_remote_copy(
                    src_ref=pair,
                    dst_ref=pair,
                    send_sem=fold_send.at[hop],
                    recv_sem=fold_recv.at[hop],
                    device_id=(lax.rem(rep + d, reps), me),
                    device_id_type=MESH,
                ).start()

    def folded(hop):
        if direct:
            settle(recv.at[hop, pl.ds(0, direct * ys * cs)], halo_recv.at[hop, 0])
        settle(recv.at[hop, pl.ds(0, (reps - 1) * (zs - direct) * cs)], fold_recv.at[hop])

    gather(0)

    for load in loads[2:5]:
        load.wait()
    positions = row_tiles * col_tiles
    line = lax.broadcasted_iota(jnp.int32, marks.shape[1:], 0)
    mark = jnp.zeros(marks.shape[1:], F32)
    for slot in range(slots):
        where = row_ref[slot] * col_tiles + col_ref[slot]
        where = jnp.where(slot < live_ref[0, 0], where + slot * positions, -1)
        mark = jnp.where(line == where, 1.0, mark)
    marks[rep] = mark

    def place(source, slot, fresh=False):
        chunk = 128
        for r in range(row_tiles):
            for c in range(col_tiles):
                which = slot * positions + r * col_tiles + c
                here = marks[source, pl.ds(which, 1), :]
                here = jnp.concatenate([here] * (side // here.shape[1]), axis=1)
                here = jnp.broadcast_to(here, (16, side)).astype(BF)
                here = jnp.concatenate([here] * (chunk // 16), axis=0)
                for i in range(0, side, chunk):
                    value = tiles_all[source, slot, i : i + chunk, :] * here
                    to = (slice(r * side + i, r * side + i + chunk), slice(c * side, (c + 1) * side))
                    block[to] = value if fresh else block[to] + value

    loads[5].wait()
    place(rep, 0, fresh=True)
    place(rep, 1)

    def tile_to(d, source, slot, ref):
        pltpu.make_async_remote_copy(
            src_ref=ref.at[slot], dst_ref=tiles_all.at[source, slot], send_sem=tile_send,
            recv_sem=tile_recv.at[lax.rem(source - rep - d + 2 * reps, reps), slot],
            device_id=(lax.rem(rep + d, reps), me), device_id_type=MESH,
        ).start()

    pl.semaphore_wait(barrier, messages + reps - 1 - jnp.where(rep == 0, 1, 0))
    for d in far_x:
        pltpu.make_async_remote_copy(
            src_ref=marks.at[rep], dst_ref=marks.at[rep], send_sem=mark_send, recv_sem=mark_recv,
            device_id=(lax.rem(rep + d, reps), me), device_id_type=MESH,
        ).start()
    exchange(0)
    left, right = lax.rem(rep + reps - 1, reps), lax.rem(rep + 1, reps)
    tile_to(1, rep, 0, tiles_hbm)
    if reps == 2:
        tile_to(1, rep, 1, tiles_hbm)
    else:
        tile_to(reps - 1, rep, 1, tiles_hbm)
        tile_to(1, rep, 1, tiles_hbm)
        tile_to(reps - 1, rep, 0, tiles_hbm)

    for load in loads[6:]:
        load.wait()
    others = pl.ds(0, reps - 1)
    settle(marks.at[others], mark_recv)
    todo = list(reversed(range(len(batches))))
    if reps == 2:
        for slot in range(slots):
            settle(tiles_all.at[0, 0], tile_recv.at[1, slot])
            place(left, slot)
    else:
        settle(tiles_all.at[0, 0], tile_recv.at[reps - 1, 0])
        tile_to(1, left, 0, tiles_all.at[left])
        settle(tiles_all.at[0, 0], tile_recv.at[1, 1])
        tile_to(reps - 1, right, 1, tiles_all.at[right])
        for source, slot in ((left, 0), (right, 1)):
            if todo:
                fold(0, todo.pop(0))
            place(source, slot)
        for source, slot, n in ((left, 1, reps - 1), (right, 0, 1)):
            if todo:
                fold(0, todo.pop(0))
            settle(tiles_all.at[0, 0], tile_recv.at[n, slot])
            place(source, slot)
    for b in todo:
        fold(0, b)
    if reps == 4:
        for slot in range(slots):
            settle(tiles_all.at[0, 0], tile_recv.at[2, slot])
            place(lax.rem(rep + 2, reps), slot)
    for c in range(own_tiles, col_tiles):
        q = c - own_tiles
        columns = min(2 * side, wide.shape[1])
        wide[:, q * 2 * side : q * 2 * side + columns] = jnp.dot(
            block[:, c * side : (c + 1) * side], spread[:, :columns], preferred_element_type=F32
        ).astype(BF)

    def own_part():
        for first in range(0, nodes, rows):
            total[first : first + rows, :] = jnp.dot(
                block[first : first + rows, :nodes], cur[...], preferred_element_type=F32
            ) + cur[first : first + rows, :].astype(F32)

    rows = 256
    for hop in range(HOPS):
        if hop:
            gather(hop)
            exchange(hop)
        own_part()
        if hop:
            for b in reversed(range(len(batches))):
                fold(hop, b)
        folded(hop)
        came = recv[hop].reshape(total_lines, half)
        low = came * half_mask[...]
        both = jnp.concatenate([low, came - low], axis=1)
        for first in range(0, nodes, rows):
            here = slice(first, first + rows)
            mixed = total[here, :] + jnp.dot(wide[here, :], both, preferred_element_type=F32)
            scale = lax.rsqrt(jnp.mean(mixed * mixed, axis=-1, keepdims=True) + 1e-06)
            normed = (mixed * scale * gain_ref[hop : hop + 1, :]).astype(BF)
            inner = jax.nn.gelu(jnp.dot(normed, win[hop], preferred_element_type=F32)).astype(BF)
            result = (mixed + jnp.dot(inner, wout[hop], preferred_element_type=F32)).astype(BF)
            if hop == HOPS - 1:
                out_ref[here, :] = result
            else:
                cur[here, :] = result

    for hop in range(HOPS):

        @pl.when(rep == 0)
        def _(hop=hop):
            settle(sent.at[hop, pl.ds(0, messages - 1)], halo_send.at[hop])

        @pl.when(rep != 0)
        def _(hop=hop):
            settle(sent.at[hop, pl.ds(0, messages)], halo_send.at[hop])

        settle(recv.at[hop, pl.ds(0, (reps - 1) * (zs - direct) * cs)], fold_send.at[hop])
    settle(marks.at[others], mark_send)
    sent_tiles = tiles_all.at[others] if reps == 4 else tiles_all.at[pl.ds(0, 1)]
    settle(sent_tiles, tile_send)


def per_device(reps, owners, features, tiles, tile_row, tile_col, tile_live, send_index, gain, w_in, w_out):
    nodes, width = features.shape
    slots, side = tiles.shape[2], tiles.shape[-1]
    halo = send_index.shape[2]
    halo_pad = (owners * halo + side - 1) // side * side
    columns = nodes + halo_pad
    lines = owners * 2 * halo
    positions = (nodes // side) * (columns // side)
    mark_lines = (slots * positions + 7) // 8 * 8
    batches = len(batches_of(plane_of(owners)[1])[1])
    vmem = pl.BlockSpec(memory_space=pltpu.VMEM)
    hbm = pl.BlockSpec(memory_space=pltpu.HBM)
    dma = pltpu.SemaphoreType.DMA
    return pl.pallas_call(
        functools.partial(kernel, reps, owners),
        out_shape=pltpu.VMEM((nodes, width), BF),
        in_specs=[hbm] * 9,
        out_specs=vmem,
        scratch_shapes=[
            pltpu.SMEM((slots,), jnp.int32),
            pltpu.SMEM((slots,), jnp.int32),
            pltpu.SMEM((1, 1), jnp.int32),
            pltpu.VMEM((halo, owners), jnp.int32),
            pltpu.VMEM(gain.shape, F32),
            pltpu.VMEM((owners, 2 * halo), jnp.int32),
            pltpu.VMEM((nodes, width), BF),
            pltpu.VMEM((lines, nodes), BF),
            pltpu.VMEM((HOPS, owners, 2 * halo, width // 2), BF),
            pltpu.VMEM((HOPS, owners, 2 * halo, width // 2), BF),
            pltpu.VMEM((lines, width // 2), BF),
            pltpu.VMEM((side, 2 * side), BF),
            pltpu.VMEM((reps, slots, side, side), BF),
            pltpu.VMEM((reps, mark_lines, 128), F32),
            pltpu.VMEM((nodes, columns), BF),
            pltpu.VMEM((nodes, lines), BF),
            pltpu.VMEM((nodes, width), F32),
            pltpu.VMEM(w_in.shape, BF),
            pltpu.VMEM(w_out.shape, BF),
            dma((9,)),
            dma,
            dma((reps, slots)),
            dma,
            dma,
            dma((HOPS,)),
            dma((HOPS, batches + 1)),
            dma((HOPS,)),
            dma((HOPS,)),
        ],
        compiler_params=pltpu.CompilerParams(
            collective_id=0, has_side_effects=True, vmem_limit_bytes=63 * 1024 * 1024
        ),
    )(
        features, tiles[0, 0], tile_row[0, 0], tile_col[0, 0], tile_live, jnp.transpose(send_index[0]), gain, w_in, w_out
    )


def solution(mesh):
    placed = (
        P("rows", None),
        P("rows", "rep", None, None, None),
        P("rows", "rep", None),
        P("rows", "rep", None),
        P("rows", "rep"),
        P("rows", None, None),
        P(),
        P(),
        P(),
    )
    body = functools.partial(per_device, mesh.shape["rep"], mesh.shape["rows"])
    return jax.shard_map(body, mesh=mesh, in_specs=placed, out_specs=P("rows", None), check_vma=False)
```

```python
import functools

import jax
import jax.numpy as jnp
from jax import lax
from jax.experimental import pallas as pl
from jax.experimental.pallas import tpu as pltpu
from jax.sharding import PartitionSpec as P

HOPS = 3
ENDS = (0, 3, 7, 11, 16)
MESH = pl.DeviceIdType.MESH
BF = jnp.bfloat16
F32 = jnp.float32


def plane_of(reps, owners):
    cores = 2 if owners >= 4 * reps else 1
    return reps, owners // (reps * cores), cores


def batches_of(zs):
    ends = ENDS if zs == ENDS[-1] else (0, zs)
    return tuple(zip(ends[:-1], ends[1:]))


def kernel(
    reps, owners, feat_hbm, tiles_hbm, row_hbm, col_hbm, live_hbm, index_hbm, gain_hbm, win_hbm, wout_hbm,
    out_ref,
    row_ref, col_ref, live_ref, index_ref, gain_ref,
    index_t, cur, pick, sent, recv, half_mask, spread, tiles_all, marks, block, wide, total, win, wout,
    load_sem, tile_send, tile_recv, mark_send, mark_recv, halo_send, halo_recv, fold_send, fold_recv,
):
    ys, zs, cs = plane_of(reps, owners)
    batches = batches_of(zs)
    rep = lax.axis_index("rep")
    me = lax.axis_index("rows")
    my_y, my_z, my_c = me // (zs * cs), (me // cs) % zs, me % cs
    nodes, width = feat_hbm.shape
    side = tiles_hbm.shape[-1]
    slots = tiles_hbm.shape[0]
    halo = index_hbm.shape[0]
    half = width // 2
    group = 2 * halo
    row_tiles = nodes // side
    col_tiles = block.shape[1] // side
    own_tiles = nodes // side
    far_y = sorted(range(ys), key=lambda d: -min(d, ys - d))
    far_x = sorted(range(1, reps), key=lambda d: -min(d, reps - d))

    barrier = pltpu.get_barrier_semaphore()

    def at(sign, dz, dy, dc):
        y = lax.rem(my_y + sign * dy + ys, ys)
        z = lax.rem(my_z + sign * dz + zs, zs)
        c = lax.rem(my_c + sign * dc + cs, cs)
        return (y * zs + z) * cs + c

    def step_of(j):
        return zs // 2 + (1 - 2 * lax.rem(j, 2)) * ((j + 1) // 2)

    def my_dy(dz):
        return lax.rem(rep + ys * zs - dz, ys)

    def partners(sign, visit):
        for b, (low, high) in enumerate(batches):
            if min(high, zs - 1) > low:

                @pl.loop(low, min(high, zs - 1))
                def _(j, b=b):
                    dz = step_of(j)
                    for dc in reversed(range(cs)):
                        visit(at(sign, dz, my_dy(dz), dc), j * 2 + dc, b)

        base = (zs - 1) * 2
        for dc in reversed(range(1, cs)):
            visit(at(sign, 0, my_dy(0), dc), base + dc, len(batches) - 1)

        @pl.when(rep != 0)
        def _():
            visit(at(sign, 0, my_dy(0), 0), base, len(batches) - 1)

    messages = zs * cs

    def greet(owner, place, b):
        pl.semaphore_signal(barrier, inc=1, device_id=(rep, owner), device_id_type=MESH)

    partners(-1, greet)
    for d in far_x:
        pl.semaphore_signal(
            barrier, inc=1, device_id=(lax.rem(rep + d, reps), me), device_id_type=MESH
        )

    loads = [
        pltpu.make_async_copy(source, to, load_sem.at[n])
        for n, (source, to) in enumerate(
            (
                (index_hbm, index_ref), (feat_hbm, cur), (row_hbm, row_ref), (col_hbm, col_ref), (live_hbm, live_ref),
                (tiles_hbm, tiles_all.at[rep]), (gain_hbm, gain_ref), (win_hbm, win), (wout_hbm, wout),
            )
        )
    ]
    for load in loads:
        load.start()

    loads[0].wait()
    index_t[...] = jnp.transpose(jnp.concatenate([index_ref[...]] * 2, axis=0))
    lane = lax.broadcasted_iota(jnp.int32, (group, group), 1)
    sub = lax.broadcasted_iota(jnp.int32, (group, group), 0)
    node = lax.broadcasted_iota(jnp.int32, (group, nodes), 1)

    def choose(owner):
        wanted = jnp.broadcast_to(index_t[pl.ds(owner, 1), :], (group, group))
        wanted = jnp.sum(jnp.where(lane == sub, wanted, 0), axis=1, keepdims=True)
        return jnp.where(node == wanted, 1.0, 0.0).astype(F32)

    for j in range(zs):
        dz = step_of(jnp.int32(j))
        rows = [choose(at(1, dz, my_dy(dz), dc)) for dc in range(cs)]
        rows += [rows[-1]] * (2 - cs)
        pick[j * 2 * group : (j + 1) * 2 * group, :] = jnp.concatenate(rows, axis=0).astype(BF)

    loads[1].wait()

    def gather(hop):
        got_lines = zs * 2 * group
        step = 256
        for first in range(0, got_lines, step):
            step = min(step, got_lines - first)
            got = jnp.dot(pick[first : first + step, :], cur[...], preferred_element_type=F32)
            line = lax.rem(lax.broadcasted_iota(jnp.int32, (step, half), 0), group)
            message = jnp.where(line < halo, got[:, :half], got[:, half:])
            sent[hop, first // group : (first + step) // group] = message.astype(BF).reshape(
                step // group, group, half
            )

    def exchange(hop):
        def send(owner, place, b):
            pltpu.make_async_remote_copy(
                src_ref=sent.at[hop, place],
                dst_ref=recv.at[hop, me],
                send_sem=halo_send.at[hop],
                recv_sem=halo_recv.at[hop, b],
                device_id=(rep, owner),
                device_id_type=MESH,
            ).start()

        partners(1, send)

        @pl.when(rep == 0)
        def _():
            pltpu.make_async_copy(
                sent.at[hop, (zs - 1) * 2], recv.at[hop, me], halo_recv.at[hop, len(batches) - 1]
            ).start()

    def settle(ref, sem):
        pltpu.make_async_copy(ref, ref, sem).wait()

    def fold(hop, b):
        low, high = batches[b]
        settle(recv.at[hop, pl.ds(0, (high - low) * cs)], halo_recv.at[hop, b])

        @pl.loop(low, high)
        def _(j):
            dz = step_of(j)
            y = lax.rem(my_y - my_dy(dz) + ys, ys)
            z = lax.rem(my_z - dz + zs, zs)
            pair = recv.at[hop, pl.ds((y * zs + z) * cs, cs)]
            for d in far_x:
                pltpu.make_async_remote_copy(
                    src_ref=pair,
                    dst_ref=pair,
                    send_sem=fold_send.at[hop],
                    recv_sem=fold_recv.at[hop],
                    device_id=(lax.rem(rep + d, reps), me),
                    device_id_type=MESH,
                ).start()

    folds = (reps - 1) * messages

    def finish_sends(hop):
        @pl.when(rep == 0)
        def _():
            settle(sent.at[hop, pl.ds(0, messages - 1)], halo_send.at[hop])

        @pl.when(rep != 0)
        def _():
            settle(sent.at[hop, pl.ds(0, messages)], halo_send.at[hop])

        settle(recv.at[hop, pl.ds(0, folds)], fold_send.at[hop])

    gather(0)

    for load in loads[2:5]:
        load.wait()
    positions = row_tiles * col_tiles
    line = lax.broadcasted_iota(jnp.int32, marks.shape[1:], 0)
    mark = jnp.zeros(marks.shape[1:], F32)
    for slot in range(slots):
        where = row_ref[slot] * col_tiles + col_ref[slot]
        where = jnp.where(slot < live_ref[0, 0], where + slot * positions, -1)
        mark = jnp.where(line == where, 1.0, mark)
    marks[rep] = mark

    def place(source, slot, fresh=False):
        chunk = 128
        for r in range(row_tiles):
            for c in range(col_tiles):
                which = slot * positions + r * col_tiles + c
                here = marks[source, pl.ds(which, 1), :]
                here = jnp.concatenate([here] * (side // here.shape[1]), axis=1)
                here = jnp.broadcast_to(here, (16, side)).astype(BF)
                here = jnp.concatenate([here] * (chunk // 16), axis=0)
                for i in range(0, side, chunk):
                    value = tiles_all[source, slot, i : i + chunk, :] * here
                    to = (slice(r * side + i, r * side + i + chunk), slice(c * side, (c + 1) * side))
                    block[to] = value if fresh else block[to] + value

    def tile_to(d, source, slot, ref):
        pltpu.make_async_remote_copy(
            src_ref=ref.at[slot], dst_ref=tiles_all.at[source, slot], send_sem=tile_send,
            recv_sem=tile_recv.at[lax.rem(source - rep - d + 2 * reps, reps), slot],
            device_id=(lax.rem(rep + d, reps), me), device_id_type=MESH,
        ).start()

    left, right = lax.rem(rep + reps - 1, reps), lax.rem(rep + 1, reps)
    pl.semaphore_wait(barrier, messages + reps - 1 - jnp.where(rep == 0, 1, 0))
    for d in far_x:
        pltpu.make_async_remote_copy(
            src_ref=marks.at[rep], dst_ref=marks.at[rep], send_sem=mark_send, recv_sem=mark_recv,
            device_id=(lax.rem(rep + d, reps), me), device_id_type=MESH,
        ).start()
    tile_to(1, rep, 0, tiles_hbm)
    if reps == 2:
        tile_to(1, rep, 1, tiles_hbm)
    else:
        tile_to(reps - 1, rep, 1, tiles_hbm)
        tile_to(1, rep, 1, tiles_hbm)
        tile_to(reps - 1, rep, 0, tiles_hbm)
    exchange(0)

    total_lines = owners * group
    lines = lax.broadcasted_iota(jnp.int32, (total_lines, half), 0)
    half_mask[...] = jnp.where(lax.rem(lines, group) < halo, 1.0, 0.0).astype(BF)
    x = lax.broadcasted_iota(jnp.int32, spread.shape, 0)
    y = lax.broadcasted_iota(jnp.int32, spread.shape, 1)
    same = (x // halo == y // group) & (lax.rem(x, halo) == lax.rem(y, halo))
    spread[...] = jnp.where(same, 1.0, 0.0).astype(BF)

    loads[5].wait()
    place(rep, 0, fresh=True)
    place(rep, 1)

    for load in loads[6:]:
        load.wait()
    others = pl.ds(0, reps - 1)
    settle(marks.at[others], mark_recv)
    todo = list(reversed(range(len(batches))))
    if reps == 2:
        for slot in range(slots):
            settle(tiles_all.at[0, 0], tile_recv.at[1, slot])
            place(left, slot)
    else:
        settle(tiles_all.at[0, 0], tile_recv.at[reps - 1, 0])
        tile_to(1, left, 0, tiles_all.at[left])
        settle(tiles_all.at[0, 0], tile_recv.at[1, 1])
        tile_to(reps - 1, right, 1, tiles_all.at[right])
        for source, slot in ((left, 0), (right, 1)):
            if todo:
                fold(0, todo.pop(0))
            place(source, slot)
        for source, slot, n in ((left, 1, reps - 1), (right, 0, 1)):
            if todo:
                fold(0, todo.pop(0))
            settle(tiles_all.at[0, 0], tile_recv.at[n, slot])
            place(source, slot)
    for b in todo:
        fold(0, b)
    if reps == 4:
        for slot in range(slots):
            settle(tiles_all.at[0, 0], tile_recv.at[2, slot])
            place(lax.rem(rep + 2, reps), slot)
    for c in range(own_tiles, col_tiles):
        q = c - own_tiles
        columns = min(2 * side, wide.shape[1])
        wide[:, q * 2 * side : q * 2 * side + columns] = jnp.dot(
            block[:, c * side : (c + 1) * side], spread[:, :columns], preferred_element_type=F32
        ).astype(BF)

    def own_part():
        for first in range(0, nodes, rows):
            total[first : first + rows, :] = jnp.dot(
                block[first : first + rows, :nodes], cur[...], preferred_element_type=F32
            ) + cur[first : first + rows, :].astype(F32)

    rows = 256
    for hop in range(HOPS):
        if hop:
            gather(hop)
            exchange(hop)
        own_part()
        if hop:
            for b in reversed(range(len(batches))):
                fold(hop, b)
            finish_sends(hop - 1)
        if hop == HOPS - 1:
            settle(marks.at[others], mark_send)
            settle(tiles_all.at[others] if reps == 4 else tiles_all.at[pl.ds(0, 1)], tile_send)
        settle(recv.at[hop, pl.ds(0, folds)], fold_recv.at[hop])
        came = recv[hop].reshape(total_lines, half)
        low = came * half_mask[...]
        both = jnp.concatenate([low, came - low], axis=1)
        parts = [slice(first, first + rows) for first in range(0, nodes, rows)]
        mixed, normed, inner = [], [], []
        for here in parts:
            mixed.append(total[here, :] + jnp.dot(wide[here, :], both, preferred_element_type=F32))
        for value in mixed:
            scale = lax.rsqrt(jnp.mean(value * value, axis=-1, keepdims=True) + 1e-06)
            normed.append((value * scale * gain_ref[hop : hop + 1, :]).astype(BF))
        for value in normed:
            inner.append(jax.nn.gelu(jnp.dot(value, win[hop], preferred_element_type=F32)).astype(BF))
        for n, here in enumerate(parts):
            result = mixed[n] + jnp.dot(inner[n], wout[hop], preferred_element_type=F32)
            if hop == HOPS - 1:
                out_ref[here, :] = result.astype(BF)
            else:
                cur[here, :] = result.astype(BF)

    finish_sends(HOPS - 1)


def per_device(reps, owners, features, tiles, tile_row, tile_col, tile_live, send_index, gain, w_in, w_out):
    nodes, width = features.shape
    slots, side = tiles.shape[2], tiles.shape[-1]
    halo = send_index.shape[2]
    halo_pad = (owners * halo + side - 1) // side * side
    columns = nodes + halo_pad
    lines = owners * 2 * halo
    positions = (nodes // side) * (columns // side)
    mark_lines = (slots * positions + 7) // 8 * 8
    _, zs, _ = plane_of(reps, owners)
    batches = len(batches_of(zs))
    pieces = zs * 2
    vmem = pl.BlockSpec(memory_space=pltpu.VMEM)
    hbm = pl.BlockSpec(memory_space=pltpu.HBM)
    dma = pltpu.SemaphoreType.DMA
    return pl.pallas_call(
        functools.partial(kernel, reps, owners),
        out_shape=pltpu.VMEM((nodes, width), BF),
        in_specs=[hbm] * 4 + [pl.BlockSpec(memory_space=pl.ANY)] + [hbm] * 4,
        out_specs=vmem,
        scratch_shapes=[
            pltpu.SMEM((slots,), jnp.int32),
            pltpu.SMEM((slots,), jnp.int32),
            pltpu.SMEM((1, 1), jnp.int32),
            pltpu.VMEM((halo, owners), jnp.int32),
            pltpu.VMEM(gain.shape, F32),
            pltpu.VMEM((owners, 2 * halo), jnp.int32),
            pltpu.VMEM((nodes, width), BF),
            pltpu.VMEM((pieces * 2 * halo, nodes), BF),
            pltpu.VMEM((HOPS, pieces, 2 * halo, width // 2), BF),
            pltpu.VMEM((HOPS, owners, 2 * halo, width // 2), BF),
            pltpu.VMEM((lines, width // 2), BF),
            pltpu.VMEM((side, 2 * side), BF),
            pltpu.VMEM((reps, slots, side, side), BF),
            pltpu.VMEM((reps, mark_lines, 128), F32),
            pltpu.VMEM((nodes, columns), BF),
            pltpu.VMEM((nodes, lines), BF),
            pltpu.VMEM((nodes, width), F32),
            pltpu.VMEM(w_in.shape, BF),
            pltpu.VMEM(w_out.shape, BF),
            dma((9,)),
            dma,
            dma((reps, slots)),
            dma,
            dma,
            dma((HOPS,)),
            dma((HOPS, batches)),
            dma((HOPS,)),
            dma((HOPS,)),
        ],
        compiler_params=pltpu.CompilerParams(
            collective_id=0, has_side_effects=True, vmem_limit_bytes=63 * 1024 * 1024
        ),
    )(
        features, tiles[0, 0], tile_row[0, 0], tile_col[0, 0], tile_live, jnp.transpose(send_index[0]), gain, w_in, w_out
    )


def solution(mesh):
    placed = (
        P("rows", None),
        P("rows", "rep", None, None, None),
        P("rows", "rep", None),
        P("rows", "rep", None),
        P("rows", "rep"),
        P("rows", None, None),
        P(),
        P(),
        P(),
    )
    body = functools.partial(per_device, mesh.shape["rep"], mesh.shape["rows"])
    return jax.shard_map(body, mesh=mesh, in_specs=placed, out_specs=P("rows", None), check_vma=False)
```

```python
import functools

import jax
import jax.numpy as jnp
from jax import lax
from jax.experimental import pallas as pl
from jax.experimental.pallas import tpu as pltpu
from jax.sharding import PartitionSpec as P

HOPS = 3
ENDS = ((0, 3, 9), (0, 3, 7, 13), (0, 3, 7, 13))
MESH = pl.DeviceIdType.MESH
BF = jnp.bfloat16
F32 = jnp.float32


def plane_of(reps, owners):
    cores = 2 if owners >= 4 * reps else 1
    return reps, owners // (reps * cores), cores


def batches_of(zs):
    every = ENDS if zs == 16 else ((0, zs - 1),) * HOPS
    return [tuple(zip(ends[:-1], ends[1:])) for ends in every]


def kernel(
    reps, owners, feat_hbm, tiles_hbm, row_hbm, col_hbm, live_hbm, index_hbm, gain_hbm, win_hbm, wout_hbm,
    out_ref,
    row_ref, col_ref, live_ref, index_ref, gain_ref,
    index_t, cur, pick, sent, recv, half_mask, spread, tiles_all, marks, block, wide, total, win, wout,
    load_sem, tile_send, tile_recv, mark_send, mark_recv, halo_send, halo_recv, fold_send, fold_recv,
):
    ys, zs, cs = plane_of(reps, owners)
    batches = batches_of(zs)
    near = [groups[-1][1] for groups in batches]
    nearest = min(near)
    rep = lax.axis_index("rep")
    me = lax.axis_index("rows")
    my_y, my_z, my_c = me // (zs * cs), (me // cs) % zs, me % cs
    nodes, width = feat_hbm.shape
    side = tiles_hbm.shape[-1]
    slots = tiles_hbm.shape[0]
    halo = index_hbm.shape[0]
    half = width // 2
    group = 2 * halo
    row_tiles = nodes // side
    col_tiles = block.shape[1] // side
    own_tiles = nodes // side
    far_y = sorted(range(ys), key=lambda d: -min(d, ys - d))
    far_x = sorted(range(1, reps), key=lambda d: -min(d, reps - d))

    barrier = pltpu.get_barrier_semaphore()

    def at(sign, dz, dy, dc):
        y = lax.rem(my_y + sign * dy + ys, ys)
        z = lax.rem(my_z + sign * dz + zs, zs)
        c = lax.rem(my_c + sign * dc + cs, cs)
        return (y * zs + z) * cs + c

    def step_of(j):
        return zs // 2 + (1 - 2 * lax.rem(j, 2)) * ((j + 1) // 2)

    def my_dy(dz):
        return lax.rem(rep + ys * zs - dz, ys)

    def place_of(j, more):
        return 2 * (zs + (zs - 1 - j) * (ys - 1) + more - 1 if more else j)

    def partners(sign, hop, visit):
        for b, (low, high) in enumerate(batches[hop]):

            @pl.loop(low, high)
            def _(j, b=b):
                dz = step_of(j)
                for dc in reversed(range(cs)):
                    visit(at(sign, dz, my_dy(dz), dc), place_of(j, 0) + dc, b)

        last = len(batches[hop])
        if near[hop] < zs - 1:

            @pl.loop(near[hop], zs - 1)
            def _(j):
                dz = step_of(j)
                for more in range(ys):
                    for dc in reversed(range(cs)):
                        owner = at(sign, dz, lax.rem(my_dy(dz) + more, ys), dc)
                        visit(owner, place_of(j, more) + dc, last)

        for more in range(ys):
            dy = lax.rem(my_dy(0) + more, ys)
            for dc in reversed(range(1, cs)):
                visit(at(sign, 0, dy, dc), place_of(zs - 1, more) + dc, last)

            @pl.when(dy != 0)
            def _(dy=dy, more=more):
                visit(at(sign, 0, dy, 0), place_of(zs - 1, more), last)

    def messages(hop):
        return (near[hop] + (zs - near[hop]) * ys) * cs - 1

    widest = near.index(nearest)

    def greet(owner, place, b):
        pl.semaphore_signal(barrier, inc=1, device_id=(rep, owner), device_id_type=MESH)

    partners(-1, widest, greet)
    for d in far_x:
        pl.semaphore_signal(
            barrier, inc=1, device_id=(lax.rem(rep + d, reps), me), device_id_type=MESH
        )

    loads = [
        pltpu.make_async_copy(source, to, load_sem.at[n])
        for n, (source, to) in enumerate(
            (
                (index_hbm, index_ref), (feat_hbm, cur), (row_hbm, row_ref), (col_hbm, col_ref), (live_hbm, live_ref),
                (tiles_hbm, tiles_all.at[rep]), (gain_hbm, gain_ref), (win_hbm, win), (wout_hbm, wout),
            )
        )
    ]
    for load in loads:
        load.start()

    loads[0].wait()
    index_t[...] = jnp.transpose(jnp.concatenate([index_ref[...]] * 2, axis=0))
    lane = lax.broadcasted_iota(jnp.int32, (group, group), 1)
    sub = lax.broadcasted_iota(jnp.int32, (group, group), 0)
    node = lax.broadcasted_iota(jnp.int32, (group, nodes), 1)

    def choose(owner):
        wanted = jnp.broadcast_to(index_t[pl.ds(owner, 1), :], (group, group))
        wanted = jnp.sum(jnp.where(lane == sub, wanted, 0), axis=1, keepdims=True)
        return jnp.where(node == wanted, 1.0, 0.0).astype(F32)

    for j in range(zs):
        dz = step_of(jnp.int32(j))
        for more in range(ys if j >= nearest else 1):
            dy = lax.rem(my_dy(dz) + more, ys)
            rows = [choose(at(1, dz, dy, dc)) for dc in range(cs)]
            rows += [rows[-1]] * (2 - cs)
            to = place_of(j, more) * group
            pick[to : to + 2 * group, :] = jnp.concatenate(rows, axis=0).astype(BF)

    loads[1].wait()

    def gather(hop):
        got_lines = (zs + (zs - near[hop]) * (ys - 1)) * 2 * group
        step = 256
        for first in range(0, got_lines, step):
            step = min(step, got_lines - first)
            got = jnp.dot(pick[first : first + step, :], cur[...], preferred_element_type=F32)
            line = lax.rem(lax.broadcasted_iota(jnp.int32, (step, half), 0), group)
            message = jnp.where(line < halo, got[:, :half], got[:, half:])
            sent[hop, first // group : (first + step) // group] = message.astype(BF).reshape(
                step // group, group, half
            )

    def exchange(hop):
        def send(owner, place, b):
            pltpu.make_async_remote_copy(
                src_ref=sent.at[hop, place],
                dst_ref=recv.at[hop, me],
                send_sem=halo_send.at[hop],
                recv_sem=halo_recv.at[hop, b],
                device_id=(rep, owner),
                device_id_type=MESH,
            ).start()

        partners(1, hop, send)

        for more in range(ys):

            @pl.when(lax.rem(my_dy(0) + more, ys) == 0)
            def _(more=more):
                pltpu.make_async_copy(
                    sent.at[hop, place_of(zs - 1, more)], recv.at[hop, me],
                    halo_recv.at[hop, len(batches[hop])],
                ).start()

    def settle(ref, sem):
        pltpu.make_async_copy(ref, ref, sem).wait()

    def fold(hop, b):
        low, high = batches[hop][b]
        settle(recv.at[hop, pl.ds(0, (high - low) * cs)], halo_recv.at[hop, b])

        @pl.loop(low, high)
        def _(j):
            dz = step_of(j)
            y = lax.rem(my_y - my_dy(dz) + ys, ys)
            z = lax.rem(my_z - dz + zs, zs)
            pair = recv.at[hop, pl.ds((y * zs + z) * cs, cs)]
            for d in far_x:
                pltpu.make_async_remote_copy(
                    src_ref=pair,
                    dst_ref=pair,
                    send_sem=fold_send.at[hop],
                    recv_sem=fold_recv.at[hop],
                    device_id=(lax.rem(rep + d, reps), me),
                    device_id_type=MESH,
                ).start()

    def folds(hop):
        return (reps - 1) * near[hop] * cs

    def finish_sends(hop):
        settle(recv.at[hop, pl.ds(0, messages(hop))], halo_send.at[hop])
        settle(recv.at[hop, pl.ds(0, folds(hop))], fold_send.at[hop])

    gather(0)

    for load in loads[2:5]:
        load.wait()
    positions = row_tiles * col_tiles
    line = lax.broadcasted_iota(jnp.int32, marks.shape[1:], 0)
    mark = jnp.zeros(marks.shape[1:], F32)
    for slot in range(slots):
        where = row_ref[slot] * col_tiles + col_ref[slot]
        where = jnp.where(slot < live_ref[0, 0], where + slot * positions, -1)
        mark = jnp.where(line == where, 1.0, mark)
    marks[rep] = mark

    def place(source, slot, fresh=False):
        chunk = 128
        for r in range(row_tiles):
            for c in range(col_tiles):
                which = slot * positions + r * col_tiles + c
                here = marks[source, pl.ds(which, 1), :]
                here = jnp.concatenate([here] * (side // here.shape[1]), axis=1)
                here = jnp.broadcast_to(here, (16, side)).astype(BF)
                here = jnp.concatenate([here] * (chunk // 16), axis=0)
                for i in range(0, side, chunk):
                    value = tiles_all[source, slot, i : i + chunk, :] * here
                    to = (slice(r * side + i, r * side + i + chunk), slice(c * side, (c + 1) * side))
                    block[to] = value if fresh else block[to] + value

    def tile_to(d, source, slot, ref):
        pltpu.make_async_remote_copy(
            src_ref=ref.at[slot], dst_ref=tiles_all.at[source, slot], send_sem=tile_send,
            recv_sem=tile_recv.at[lax.rem(source - rep - d + 2 * reps, reps), slot],
            device_id=(lax.rem(rep + d, reps), me), device_id_type=MESH,
        ).start()

    left, right = lax.rem(rep + reps - 1, reps), lax.rem(rep + 1, reps)
    pl.semaphore_wait(barrier, messages(widest) + reps - 1)
    for d in far_x:
        pltpu.make_async_remote_copy(
            src_ref=marks.at[rep], dst_ref=marks.at[rep], send_sem=mark_send, recv_sem=mark_recv,
            device_id=(lax.rem(rep + d, reps), me), device_id_type=MESH,
        ).start()
    tile_to(1, rep, 0, tiles_hbm)
    if reps == 2:
        tile_to(1, rep, 1, tiles_hbm)
    else:
        tile_to(reps - 1, rep, 1, tiles_hbm)
        tile_to(1, rep, 1, tiles_hbm)
        tile_to(reps - 1, rep, 0, tiles_hbm)
    exchange(0)

    total_lines = owners * group
    lines = lax.broadcasted_iota(jnp.int32, (total_lines, half), 0)
    half_mask[...] = jnp.where(lax.rem(lines, group) < halo, 1.0, 0.0).astype(BF)
    x = lax.broadcasted_iota(jnp.int32, spread.shape, 0)
    y = lax.broadcasted_iota(jnp.int32, spread.shape, 1)
    same = (x // halo == y // group) & (lax.rem(x, halo) == lax.rem(y, halo))
    spread[...] = jnp.where(same, 1.0, 0.0).astype(BF)

    loads[5].wait()
    place(rep, 0, fresh=True)
    place(rep, 1)

    for load in loads[6:]:
        load.wait()
    others = pl.ds(0, reps - 1)
    settle(marks.at[others], mark_recv)
    todo = list(reversed(range(len(batches[0]))))
    if reps == 2:
        for slot in range(slots):
            settle(tiles_all.at[0, 0], tile_recv.at[1, slot])
            place(left, slot)
    else:
        settle(tiles_all.at[0, 0], tile_recv.at[reps - 1, 0])
        tile_to(1, left, 0, tiles_all.at[left])
        settle(tiles_all.at[0, 0], tile_recv.at[1, 1])
        tile_to(reps - 1, right, 1, tiles_all.at[right])
        for source, slot in ((left, 0), (right, 1)):
            if todo:
                fold(0, todo.pop(0))
            place(source, slot)
        for source, slot, n in ((left, 1, reps - 1), (right, 0, 1)):
            if todo:
                fold(0, todo.pop(0))
            settle(tiles_all.at[0, 0], tile_recv.at[n, slot])
            place(source, slot)
    for b in todo:
        fold(0, b)
    if reps == 4:
        for slot in range(slots):
            settle(tiles_all.at[0, 0], tile_recv.at[2, slot])
            place(lax.rem(rep + 2, reps), slot)
    for c in range(own_tiles, col_tiles):
        q = c - own_tiles
        columns = min(2 * side, wide.shape[1])
        wide[:, q * 2 * side : q * 2 * side + columns] = jnp.dot(
            block[:, c * side : (c + 1) * side], spread[:, :columns], preferred_element_type=F32
        ).astype(BF)

    def own_part():
        for first in range(0, nodes, rows):
            total[first : first + rows, :] = jnp.dot(
                block[first : first + rows, :nodes], cur[...], preferred_element_type=F32
            ) + cur[first : first + rows, :].astype(F32)

    rows = 256
    for hop in range(HOPS):
        if hop:
            gather(hop)
            exchange(hop)
        own_part()
        if hop:
            for b in reversed(range(len(batches[hop]))):
                fold(hop, b)
            finish_sends(hop - 1)
        if hop == HOPS - 1:
            settle(marks.at[others], mark_send)
            settle(tiles_all.at[others] if reps == 4 else tiles_all.at[pl.ds(0, 1)], tile_send)
        settle(recv.at[hop, pl.ds(0, (zs - near[hop]) * ys * cs)], halo_recv.at[hop, len(batches[hop])])
        settle(recv.at[hop, pl.ds(0, folds(hop))], fold_recv.at[hop])
        came = recv[hop].reshape(total_lines, half)
        low = came * half_mask[...]
        both = jnp.concatenate([low, came - low], axis=1)
        parts = [slice(first, first + rows) for first in range(0, nodes, rows)]
        mixed, normed, inner = [], [], []
        for here in parts:
            mixed.append(total[here, :] + jnp.dot(wide[here, :], both, preferred_element_type=F32))
        for value in mixed:
            scale = lax.rsqrt(jnp.mean(value * value, axis=-1, keepdims=True) + 1e-06)
            normed.append((value * scale * gain_ref[hop : hop + 1, :]).astype(BF))
        for value in normed:
            inner.append(jax.nn.gelu(jnp.dot(value, win[hop], preferred_element_type=F32)).astype(BF))
        for n, here in enumerate(parts):
            result = mixed[n] + jnp.dot(inner[n], wout[hop], preferred_element_type=F32)
            if hop == HOPS - 1:
                out_ref[here, :] = result.astype(BF)
            else:
                cur[here, :] = result.astype(BF)

    finish_sends(HOPS - 1)


def per_device(reps, owners, features, tiles, tile_row, tile_col, tile_live, send_index, gain, w_in, w_out):
    nodes, width = features.shape
    slots, side = tiles.shape[2], tiles.shape[-1]
    halo = send_index.shape[2]
    halo_pad = (owners * halo + side - 1) // side * side
    columns = nodes + halo_pad
    lines = owners * 2 * halo
    positions = (nodes // side) * (columns // side)
    mark_lines = (slots * positions + 7) // 8 * 8
    ys, zs, _ = plane_of(reps, owners)
    groups = batches_of(zs)
    batches = max(len(g) for g in groups) + 1
    pieces = (zs + (zs - min(g[-1][1] for g in groups)) * (ys - 1)) * 2
    vmem = pl.BlockSpec(memory_space=pltpu.VMEM)
    hbm = pl.BlockSpec(memory_space=pltpu.HBM)
    dma = pltpu.SemaphoreType.DMA
    return pl.pallas_call(
        functools.partial(kernel, reps, owners),
        out_shape=pltpu.VMEM((nodes, width), BF),
        in_specs=[hbm] * 4 + [pl.BlockSpec(memory_space=pl.ANY)] + [hbm] * 4,
        out_specs=vmem,
        scratch_shapes=[
            pltpu.SMEM((slots,), jnp.int32),
            pltpu.SMEM((slots,), jnp.int32),
            pltpu.SMEM((1, 1), jnp.int32),
            pltpu.VMEM((halo, owners), jnp.int32),
            pltpu.VMEM(gain.shape, F32),
            pltpu.VMEM((owners, 2 * halo), jnp.int32),
            pltpu.VMEM((nodes, width), BF),
            pltpu.VMEM((pieces * 2 * halo, nodes), BF),
            pltpu.VMEM((HOPS, pieces, 2 * halo, width // 2), BF),
            pltpu.VMEM((HOPS, owners, 2 * halo, width // 2), BF),
            pltpu.VMEM((lines, width // 2), BF),
            pltpu.VMEM((side, 2 * side), BF),
            pltpu.VMEM((reps, slots, side, side), BF),
            pltpu.VMEM((reps, mark_lines, 128), F32),
            pltpu.VMEM((nodes, columns), BF),
            pltpu.VMEM((nodes, lines), BF),
            pltpu.VMEM((nodes, width), F32),
            pltpu.VMEM(w_in.shape, BF),
            pltpu.VMEM(w_out.shape, BF),
            dma((9,)),
            dma,
            dma((reps, slots)),
            dma,
            dma,
            dma((HOPS,)),
            dma((HOPS, batches)),
            dma((HOPS,)),
            dma((HOPS,)),
        ],
        compiler_params=pltpu.CompilerParams(
            collective_id=0, has_side_effects=True, vmem_limit_bytes=63 * 1024 * 1024
        ),
    )(
        features, tiles[0, 0], tile_row[0, 0], tile_col[0, 0], tile_live, jnp.transpose(send_index[0]), gain, w_in, w_out
    )


def solution(mesh):
    placed = (
        P("rows", None),
        P("rows", "rep", None, None, None),
        P("rows", "rep", None),
        P("rows", "rep", None),
        P("rows", "rep"),
        P("rows", None, None),
        P(),
        P(),
        P(),
    )
    body = functools.partial(per_device, mesh.shape["rep"], mesh.shape["rows"])
    return jax.shard_map(body, mesh=mesh, in_specs=placed, out_specs=P("rows", None), check_vma=False)
```

```python
import functools

import jax
import jax.numpy as jnp
from jax import lax
from jax.experimental import pallas as pl
from jax.experimental.pallas import tpu as pltpu
from jax.sharding import PartitionSpec as P

HOPS = 3
ENDS = ((0, 3, 7), (0, 3, 7, 13), (0, 3, 7, 13))
MESH = pl.DeviceIdType.MESH
BF = jnp.bfloat16
F32 = jnp.float32


def plane_of(reps, owners):
    cores = 2 if owners >= 4 * reps else 1
    return reps, owners // (reps * cores), cores


def batches_of(zs):
    every = ENDS if zs == 16 else ((0, zs - 1),) * HOPS
    return [tuple(zip(ends[:-1], ends[1:])) for ends in every]


def kernel(
    reps, owners, feat_hbm, tiles_hbm, row_hbm, col_hbm, live_hbm, index_hbm, gain_hbm, win_hbm, wout_hbm,
    out_ref,
    row_ref, col_ref, live_ref, index_ref, gain_ref,
    index_t, cur, pick, sent, recv, half_mask, spread, tiles_all, marks, block, wide, total, win, wout,
    load_sem, tile_send, tile_recv, mark_send, mark_recv, halo_send, halo_recv, fold_send, fold_recv,
):
    ys, zs, cs = plane_of(reps, owners)
    batches = batches_of(zs)
    near = [groups[-1][1] for groups in batches]
    nearest = min(near)
    rep = lax.axis_index("rep")
    me = lax.axis_index("rows")
    my_y, my_z, my_c = me // (zs * cs), (me // cs) % zs, me % cs
    nodes, width = feat_hbm.shape
    side = tiles_hbm.shape[-1]
    slots = tiles_hbm.shape[0]
    halo = index_hbm.shape[0]
    half = width // 2
    group = 2 * halo
    row_tiles = nodes // side
    col_tiles = block.shape[1] // side
    own_tiles = nodes // side
    far_y = sorted(range(ys), key=lambda d: -min(d, ys - d))
    far_x = sorted(range(1, reps), key=lambda d: -min(d, reps - d))

    barrier = pltpu.get_barrier_semaphore()

    def at(sign, dz, dy, dc):
        y = lax.rem(my_y + sign * dy + ys, ys)
        z = lax.rem(my_z + sign * dz + zs, zs)
        c = lax.rem(my_c + sign * dc + cs, cs)
        return (y * zs + z) * cs + c

    def step_of(j):
        return zs // 2 + (1 - 2 * lax.rem(j, 2)) * ((j + 1) // 2)

    def my_dy(dz):
        return lax.rem(rep + ys * zs - dz, ys)

    def place_of(j, more):
        return 2 * (zs + (zs - 1 - j) * (ys - 1) + more - 1 if more else j)

    def partners(sign, hop, visit):
        for b, (low, high) in enumerate(batches[hop]):

            @pl.loop(low, high)
            def _(j, b=b):
                dz = step_of(j)
                for dc in reversed(range(cs)):
                    visit(at(sign, dz, my_dy(dz), dc), place_of(j, 0) + dc, b)

        last = len(batches[hop])
        if near[hop] < zs - 1:

            @pl.loop(near[hop], zs - 1)
            def _(j):
                dz = step_of(j)
                for more in range(ys):
                    for dc in reversed(range(cs)):
                        owner = at(sign, dz, lax.rem(my_dy(dz) + more, ys), dc)
                        visit(owner, place_of(j, more) + dc, last)

        for more in range(ys):
            dy = lax.rem(my_dy(0) + more, ys)
            for dc in reversed(range(1, cs)):
                visit(at(sign, 0, dy, dc), place_of(zs - 1, more) + dc, last)

            @pl.when(dy != 0)
            def _(dy=dy, more=more):
                visit(at(sign, 0, dy, 0), place_of(zs - 1, more), last)

    def messages(hop):
        return (near[hop] + (zs - near[hop]) * ys) * cs - 1

    widest = near.index(nearest)

    def greet(owner, place, b):
        pl.semaphore_signal(barrier, inc=1, device_id=(rep, owner), device_id_type=MESH)

    partners(-1, widest, greet)
    for d in far_x:
        pl.semaphore_signal(
            barrier, inc=1, device_id=(lax.rem(rep + d, reps), me), device_id_type=MESH
        )

    loads = [
        pltpu.make_async_copy(source, to, load_sem.at[n])
        for n, (source, to) in enumerate(
            (
                (index_hbm, index_ref), (feat_hbm, cur), (row_hbm, row_ref), (col_hbm, col_ref), (live_hbm, live_ref),
                (tiles_hbm, tiles_all.at[rep]), (gain_hbm, gain_ref), (win_hbm, win), (wout_hbm, wout),
            )
        )
    ]
    for load in loads:
        load.start()

    loads[0].wait()
    index_t[...] = jnp.transpose(jnp.concatenate([index_ref[...]] * 2, axis=0))
    lane = lax.broadcasted_iota(jnp.int32, (group, group), 1)
    sub = lax.broadcasted_iota(jnp.int32, (group, group), 0)
    node = lax.broadcasted_iota(jnp.int32, (group, nodes), 1)

    def choose(owner):
        wanted = jnp.broadcast_to(index_t[pl.ds(owner, 1), :], (group, group))
        wanted = jnp.sum(jnp.where(lane == sub, wanted, 0), axis=1, keepdims=True)
        return jnp.where(node == wanted, 1.0, 0.0).astype(F32)

    for j in range(zs):
        dz = step_of(jnp.int32(j))
        for more in range(ys if j >= nearest else 1):
            dy = lax.rem(my_dy(dz) + more, ys)
            rows = [choose(at(1, dz, dy, dc)) for dc in range(cs)]
            rows += [rows[-1]] * (2 - cs)
            to = place_of(j, more) * group
            pick[to : to + 2 * group, :] = jnp.concatenate(rows, axis=0).astype(BF)

    loads[1].wait()

    def gather(hop):
        got_lines = (zs + (zs - near[hop]) * (ys - 1)) * 2 * group
        step = 256
        for first in range(0, got_lines, step):
            step = min(step, got_lines - first)
            got = jnp.dot(pick[first : first + step, :], cur[...], preferred_element_type=F32)
            line = lax.rem(lax.broadcasted_iota(jnp.int32, (step, half), 0), group)
            message = jnp.where(line < halo, got[:, :half], got[:, half:])
            sent[hop, first // group : (first + step) // group] = message.astype(BF).reshape(
                step // group, group, half
            )

    def exchange(hop):
        def send(owner, place, b):
            pltpu.make_async_remote_copy(
                src_ref=sent.at[hop, place],
                dst_ref=recv.at[hop, me],
                send_sem=halo_send.at[hop],
                recv_sem=halo_recv.at[hop, b],
                device_id=(rep, owner),
                device_id_type=MESH,
            ).start()

        partners(1, hop, send)

        for more in range(ys):

            @pl.when(lax.rem(my_dy(0) + more, ys) == 0)
            def _(more=more):
                pltpu.make_async_copy(
                    sent.at[hop, place_of(zs - 1, more)], recv.at[hop, me],
                    halo_recv.at[hop, len(batches[hop])],
                ).start()

    def settle(ref, sem):
        pltpu.make_async_copy(ref, ref, sem).wait()

    def fold(hop, b):
        low, high = batches[hop][b]
        settle(recv.at[hop, pl.ds(0, (high - low) * cs)], halo_recv.at[hop, b])

        @pl.loop(low, high)
        def _(j):
            dz = step_of(j)
            y = lax.rem(my_y - my_dy(dz) + ys, ys)
            z = lax.rem(my_z - dz + zs, zs)
            pair = recv.at[hop, pl.ds((y * zs + z) * cs, cs)]
            for d in far_x:
                pltpu.make_async_remote_copy(
                    src_ref=pair,
                    dst_ref=pair,
                    send_sem=fold_send.at[hop],
                    recv_sem=fold_recv.at[hop],
                    device_id=(lax.rem(rep + d, reps), me),
                    device_id_type=MESH,
                ).start()

    def folds(hop):
        return (reps - 1) * near[hop] * cs

    def finish_sends(hop):
        settle(recv.at[hop, pl.ds(0, messages(hop))], halo_send.at[hop])
        settle(recv.at[hop, pl.ds(0, folds(hop))], fold_send.at[hop])

    gather(0)

    for load in loads[2:5]:
        load.wait()
    positions = row_tiles * col_tiles
    line = lax.broadcasted_iota(jnp.int32, marks.shape[1:], 0)
    mark = jnp.zeros(marks.shape[1:], F32)
    for slot in range(slots):
        where = row_ref[slot] * col_tiles + col_ref[slot]
        where = jnp.where(slot < live_ref[0, 0], where + slot * positions, -1)
        mark = jnp.where(line == where, 1.0, mark)
    marks[rep] = mark

    def place(source, slot, fresh=False):
        chunk = 128
        for r in range(row_tiles):
            for c in range(col_tiles):
                which = slot * positions + r * col_tiles + c
                here = marks[source, pl.ds(which, 1), :]
                here = jnp.concatenate([here] * (side // here.shape[1]), axis=1)
                here = jnp.broadcast_to(here, (16, side)).astype(BF)
                here = jnp.concatenate([here] * (chunk // 16), axis=0)
                for i in range(0, side, chunk):
                    value = tiles_all[source, slot, i : i + chunk, :] * here
                    to = (slice(r * side + i, r * side + i + chunk), slice(c * side, (c + 1) * side))
                    block[to] = value if fresh else block[to] + value

    def tile_piece(d, source, slot, ref, piece):
        cut = pl.ds(piece * (side // 2), side // 2)
        pltpu.make_async_remote_copy(
            src_ref=ref.at[slot, cut], dst_ref=tiles_all.at[source, slot, cut], send_sem=tile_send,
            recv_sem=tile_recv.at[lax.rem(source - rep - d + 2 * reps, reps), slot, piece],
            device_id=(lax.rem(rep + d, reps), me), device_id_type=MESH,
        ).start()

    def tile_to(d, source, slot, ref):
        for piece in range(2):
            tile_piece(d, source, slot, ref, piece)

    def await_piece(n, slot, piece):
        settle(tiles_all.at[0, 0, pl.ds(0, side // 2)], tile_recv.at[n, slot, piece])

    left, right = lax.rem(rep + reps - 1, reps), lax.rem(rep + 1, reps)
    pl.semaphore_wait(barrier, messages(widest) + reps - 1)
    for d in far_x:
        pltpu.make_async_remote_copy(
            src_ref=marks.at[rep], dst_ref=marks.at[rep], send_sem=mark_send, recv_sem=mark_recv,
            device_id=(lax.rem(rep + d, reps), me), device_id_type=MESH,
        ).start()
    tile_to(1, rep, 0, tiles_hbm)
    if reps == 2:
        tile_to(1, rep, 1, tiles_hbm)
    else:
        tile_to(reps - 1, rep, 1, tiles_hbm)
        tile_to(1, rep, 1, tiles_hbm)
        tile_to(reps - 1, rep, 0, tiles_hbm)
    exchange(0)

    total_lines = owners * group
    lines = lax.broadcasted_iota(jnp.int32, (total_lines, half), 0)
    half_mask[...] = jnp.where(lax.rem(lines, group) < halo, 1.0, 0.0).astype(BF)
    x = lax.broadcasted_iota(jnp.int32, spread.shape, 0)
    y = lax.broadcasted_iota(jnp.int32, spread.shape, 1)
    same = (x // halo == y // group) & (lax.rem(x, halo) == lax.rem(y, halo))
    spread[...] = jnp.where(same, 1.0, 0.0).astype(BF)

    loads[5].wait()
    place(rep, 0, fresh=True)
    place(rep, 1)

    for load in loads[6:]:
        load.wait()
    others = pl.ds(0, reps - 1)
    settle(marks.at[others], mark_recv)
    todo = list(reversed(range(len(batches[0]))))
    if reps == 2:
        for slot in range(slots):
            await_piece(1, slot, 0)
            await_piece(1, slot, 1)
            place(left, slot)
    else:
        for piece in range(2):
            await_piece(reps - 1, 0, piece)
            tile_piece(1, left, 0, tiles_all.at[left], piece)
            await_piece(1, 1, piece)
            tile_piece(reps - 1, right, 1, tiles_all.at[right], piece)
        for source, slot in ((left, 0), (right, 1)):
            if todo:
                fold(0, todo.pop(0))
            place(source, slot)
        for source, slot, n in ((left, 1, reps - 1), (right, 0, 1)):
            if todo:
                fold(0, todo.pop(0))
            await_piece(n, slot, 0)
            await_piece(n, slot, 1)
            place(source, slot)
    for b in todo:
        fold(0, b)
    if reps == 4:
        for slot in range(slots):
            await_piece(2, slot, 0)
            await_piece(2, slot, 1)
            place(lax.rem(rep + 2, reps), slot)
    for c in range(own_tiles, col_tiles):
        q = c - own_tiles
        columns = min(2 * side, wide.shape[1])
        wide[:, q * 2 * side : q * 2 * side + columns] = jnp.dot(
            block[:, c * side : (c + 1) * side], spread[:, :columns], preferred_element_type=F32
        ).astype(BF)

    def own_part():
        for first in range(0, nodes, rows):
            total[first : first + rows, :] = jnp.dot(
                block[first : first + rows, :nodes], cur[...], preferred_element_type=F32
            ) + cur[first : first + rows, :].astype(F32)

    rows = 256
    for hop in range(HOPS):
        if hop:
            gather(hop)
            exchange(hop)
        own_part()
        if hop:
            for b in reversed(range(len(batches[hop]))):
                fold(hop, b)
            finish_sends(hop - 1)
        if hop == HOPS - 1:
            settle(marks.at[others], mark_send)
            settle(tiles_all.at[others] if reps == 4 else tiles_all.at[pl.ds(0, 1)], tile_send)
        settle(recv.at[hop, pl.ds(0, (zs - near[hop]) * ys * cs)], halo_recv.at[hop, len(batches[hop])])
        settle(recv.at[hop, pl.ds(0, folds(hop))], fold_recv.at[hop])
        came = recv[hop].reshape(total_lines, half)
        low = came * half_mask[...]
        both = jnp.concatenate([low, came - low], axis=1)
        parts = [slice(first, first + rows) for first in range(0, nodes, rows)]
        mixed, normed, inner = [], [], []
        for here in parts:
            mixed.append(total[here, :] + jnp.dot(wide[here, :], both, preferred_element_type=F32))
        for value in mixed:
            scale = lax.rsqrt(jnp.mean(value * value, axis=-1, keepdims=True) + 1e-06)
            normed.append((value * scale * gain_ref[hop : hop + 1, :]).astype(BF))
        for value in normed:
            inner.append(jax.nn.gelu(jnp.dot(value, win[hop], preferred_element_type=F32)).astype(BF))
        for n, here in enumerate(parts):
            result = mixed[n] + jnp.dot(inner[n], wout[hop], preferred_element_type=F32)
            if hop == HOPS - 1:
                out_ref[here, :] = result.astype(BF)
            else:
                cur[here, :] = result.astype(BF)

    finish_sends(HOPS - 1)


def per_device(reps, owners, features, tiles, tile_row, tile_col, tile_live, send_index, gain, w_in, w_out):
    nodes, width = features.shape
    slots, side = tiles.shape[2], tiles.shape[-1]
    halo = send_index.shape[2]
    halo_pad = (owners * halo + side - 1) // side * side
    columns = nodes + halo_pad
    lines = owners * 2 * halo
    positions = (nodes // side) * (columns // side)
    mark_lines = (slots * positions + 7) // 8 * 8
    ys, zs, _ = plane_of(reps, owners)
    groups = batches_of(zs)
    batches = max(len(g) for g in groups) + 1
    pieces = (zs + (zs - min(g[-1][1] for g in groups)) * (ys - 1)) * 2
    vmem = pl.BlockSpec(memory_space=pltpu.VMEM)
    hbm = pl.BlockSpec(memory_space=pltpu.HBM)
    dma = pltpu.SemaphoreType.DMA
    return pl.pallas_call(
        functools.partial(kernel, reps, owners),
        out_shape=pltpu.VMEM((nodes, width), BF),
        in_specs=[hbm] * 4 + [pl.BlockSpec(memory_space=pl.ANY)] + [hbm] * 4,
        out_specs=vmem,
        scratch_shapes=[
            pltpu.SMEM((slots,), jnp.int32),
            pltpu.SMEM((slots,), jnp.int32),
            pltpu.SMEM((1, 1), jnp.int32),
            pltpu.VMEM((halo, owners), jnp.int32),
            pltpu.VMEM(gain.shape, F32),
            pltpu.VMEM((owners, 2 * halo), jnp.int32),
            pltpu.VMEM((nodes, width), BF),
            pltpu.VMEM((pieces * 2 * halo, nodes), BF),
            pltpu.VMEM((HOPS, pieces, 2 * halo, width // 2), BF),
            pltpu.VMEM((HOPS, owners, 2 * halo, width // 2), BF),
            pltpu.VMEM((lines, width // 2), BF),
            pltpu.VMEM((side, 2 * side), BF),
            pltpu.VMEM((reps, slots, side, side), BF),
            pltpu.VMEM((reps, mark_lines, 128), F32),
            pltpu.VMEM((nodes, columns), BF),
            pltpu.VMEM((nodes, lines), BF),
            pltpu.VMEM((nodes, width), F32),
            pltpu.VMEM(w_in.shape, BF),
            pltpu.VMEM(w_out.shape, BF),
            dma((9,)),
            dma,
            dma((reps, slots, 2)),
            dma,
            dma,
            dma((HOPS,)),
            dma((HOPS, batches)),
            dma((HOPS,)),
            dma((HOPS,)),
        ],
        compiler_params=pltpu.CompilerParams(
            collective_id=0, has_side_effects=True, vmem_limit_bytes=63 * 1024 * 1024
        ),
    )(
        features, tiles[0, 0], tile_row[0, 0], tile_col[0, 0], tile_live, jnp.transpose(send_index[0]), gain, w_in, w_out
    )


def solution(mesh):
    placed = (
        P("rows", None),
        P("rows", "rep", None, None, None),
        P("rows", "rep", None),
        P("rows", "rep", None),
        P("rows", "rep"),
        P("rows", None, None),
        P(),
        P(),
        P(),
    )
    body = functools.partial(per_device, mesh.shape["rep"], mesh.shape["rows"])
    return jax.shard_map(body, mesh=mesh, in_specs=placed, out_specs=P("rows", None), check_vma=False)
```
